32 devices in a mesh: gy: 8 (over y, x, core), gx: 4 (over z).
Axes of the slice: x: 2, y: 2, z: 4, core: 2. Of those that a mesh axis runs over, the one named last changes fastest.
Arguments:
- level_set: float32 [128, 8192], P('gy', 'gx'), may hold values from -6 to 6
- spread_rate: float32 [128, 8192], P('gy', 'gx'), may hold values from 0.2 to 2
- cotangent: float32 [128, 8192], P('gy', 'gx'), may hold values from -6 to 6
Outputs:
- final_state: float32 [128, 8192], P('gy', 'gx')
- rate_gradient: float32 [128, 8192], P('gy', 'gx')
- initial_gradient: float32 [128, 8192], P('gy', 'gx')
The draws below stay inside these ranges and needn't reach their ends.
All inputs are finite; a program needn't handle non-finite values.
Results may differ from the reference program's by a relative error of at most 0.000029.
Values sent between devices are 32-bit elements; how exact they have to be, the bound alone decides.
A program may use at most 128 MiB of HBM per device.

```python
import math
import jax
import jax.numpy as jnp

STEPS = 6
NY = 128
NX = 8192


def steps_of(key, dims, pieces, least, high):
    loudness, own = 1.0, jax.random.fold_in(key, 6)
    for dim, shards_of in pieces:
        steps = jnp.exp(jax.random.uniform(jax.random.fold_in(own, dim), (shards_of,), jnp.float32, least / len(pieces), high / len(pieces)))
        loudness = loudness * jnp.repeat(steps, dims[dim] // shards_of).reshape([-1 if axis == dim else 1 for axis in range(len(dims))])
    return loudness


def gaussian(rng, dims, spread, reach, shards=(), dtype=jnp.bfloat16):
    array = jax.random.normal(rng, dims, jnp.float32) * spread
    if len(shards) > 0:
        array = steps_of(rng, dims, shards, -0.22, 0.18) * array
    return jnp.clip(array, min=-reach, max=reach).astype(dtype)


def setup_inputs(seed: int = 0) -> dict:
    splits = jax.random.split(jax.random.key(seed), 4)
    level_set = gaussian(splits[0], (NY, NX), 1.0, 6.0, ((0, 8), (1, 4)), jnp.float32)
    spread_rate = jnp.clip(jnp.exp(math.log(2.0) - 2.3025851 * jax.random.uniform(splits[1], (NY, NX), jnp.float32) ** steps_of(splits[1], (NY, NX), ((0, 8), (1, 4)), -0.2, 0.2)), 0.2, 2.0)
    cotangent = gaussian(splits[2], (NY, NX), 1.0, 6.0, ((0, 8), (1, 4)), jnp.float32)
    return dict(level_set=level_set, spread_rate=spread_rate, cotangent=cotangent)


time_step = 0.2
smooth_eps = 0.001
speed_floor = 0.25

def weno(first, second, third, fourth, fifth):
    cand_one = first / 3.0 - 7.0 * second / 6.0 + 11.0 * third / 6.0
    cand_two = -second / 6.0 + 5.0 * third / 6.0 + fourth / 3.0
    cand_three = third / 3.0 + 5.0 * fourth / 6.0 - fifth / 6.0
    beta_one = 13.0 / 12.0 * (first - 2.0 * second + third) ** 2 + 0.25 * (first - 4.0 * second + 3.0 * third) ** 2
    beta_two = 13.0 / 12.0 * (second - 2.0 * third + fourth) ** 2 + 0.25 * (second - fourth) ** 2
    beta_three = 13.0 / 12.0 * (third - 2.0 * fourth + fifth) ** 2 + 0.25 * (3.0 * third - 4.0 * fourth + fifth) ** 2
    alpha_one = 0.1 / (smooth_eps + beta_one) ** 2
    alpha_two = 0.6 / (smooth_eps + beta_two) ** 2
    alpha_three = 0.3 / (smooth_eps + beta_three) ** 2
    return (alpha_one * cand_one + alpha_two * cand_two + alpha_three * cand_three) / (alpha_one + alpha_two + alpha_three)

def sides(diffs, count):
    left = weno(diffs[0:count], diffs[1:count + 1], diffs[2:count + 2], diffs[3:count + 3], diffs[4:count + 4])
    right = weno(diffs[5:count + 5], diffs[4:count + 4], diffs[3:count + 3], diffs[2:count + 2], diffs[1:count + 1])
    return (left, right)

def speed(padded):
    row_count = padded.shape[0] - 6
    col_count = padded.shape[1] - 6
    column_band = padded[:, 3:3 + col_count]
    left_y, right_y = sides(column_band[1:] - column_band[:-1], row_count)
    row_band = padded[3:3 + row_count, :]
    row_diffs = (row_band[:, 1:] - row_band[:, :-1]).T
    left_x, right_x = sides(row_diffs, col_count)
    left_x, right_x = (left_x.T, right_x.T)
    square = jnp.maximum(left_y, 0.0) ** 2 + jnp.minimum(right_y, 0.0) ** 2
    square = square + jnp.maximum(left_x, 0.0) ** 2 + jnp.minimum(right_x, 0.0) ** 2
    return jnp.sqrt(square + speed_floor)

def periodic(state):
    return jnp.pad(state, 3, mode='wrap')

def reference(level_set, spread_rate, cotangent):
    stored = []
    state = level_set
    for step in range(STEPS):
        stored.append(state)
        middle = state - time_step * spread_rate * speed(periodic(state))
        stored.append(middle)
        state = 0.5 * state + 0.5 * (middle - time_step * spread_rate * speed(periodic(middle)))
    final_state = state

    def adjoint(source, weight):
        value, pull_back = jax.vjp(speed, periodic(source))
        grad_pad, = pull_back(spread_rate * weight)
        back = grad_pad[3:-3, 3:-3]
        back = back.at[-3:, :].add(grad_pad[0:3, 3:-3])
        back = back.at[0:3, :].add(grad_pad[-3:, 3:-3])
        back = back.at[:, -3:].add(grad_pad[3:-3, 0:3])
        back = back.at[:, 0:3].add(grad_pad[3:-3, -3:])
        return (back, value)
    adjoint_state = cotangent
    rate_gradient = jnp.zeros_like(spread_rate)
    for step in reversed(range(STEPS)):
        weight_late = 0.5 * time_step * adjoint_state
        back_late, value_late = adjoint(stored[2 * step + 1], weight_late)
        adjoint_middle = 0.5 * adjoint_state - back_late
        rate_gradient = rate_gradient - weight_late * value_late
        weight_early = time_step * adjoint_middle
        back_early, value_early = adjoint(stored[2 * step], weight_early)
        rate_gradient = rate_gradient - weight_early * value_early
        adjoint_state = 0.5 * adjoint_state + adjoint_middle - back_early
    return (final_state, rate_gradient, adjoint_state)
```

```python
import functools

import jax
import jax.numpy as jnp
from jax import lax
from jax.experimental import pallas as pl
from jax.experimental.pallas import tpu as pltpu
from jax.sharding import PartitionSpec as P

STEPS = 6
STAGES = 2 * STEPS
time_step = 0.2
smooth_eps = 0.001
speed_floor = 0.25
LANES = 128
SHIFTS = (-3, -2, -1, 1, 2, 3)


def blend(m, q1, q2, q3, t1, t2, t3):
    t23 = t2 * t3
    inverse = 1.0 / (t1 * t23)
    r1 = t23 * inverse
    r2 = (t1 * t3) * inverse
    r3 = (t1 * t2) * inverse
    a1 = 0.1 * (r1 * r1)
    a2 = 0.6 * (r2 * r2)
    a3 = 0.3 * (r3 * r3)
    total = 1.0 / (a1 + a2 + a3)
    w1, w2, w3 = a1 * total, a2 * total, a3 * total
    offset = w1 * q1 + w2 * q2 + w3 * q3
    return m + offset, (offset, w1, w2, w3, r1, r2, r3, q1, q2, q3)


def values(u):
    m = [u[k + 1] - u[k] for k in range(6)]
    e = [m[k + 1] - m[k] for k in range(5)]
    sq = [x * x for x in e]
    low = [(4.0 / 3.0) * x + smooth_eps for x in sq]
    high = [(10.0 / 3.0) * x for x in sq]
    prod = [e[k] * e[k + 1] for k in range(4)]
    far = [(11.0 / 3.0) * x for x in prod]
    t1 = low[0] + high[1] - far[0]
    t2 = low[1] + (low[2] - smooth_eps) - (5.0 / 3.0) * prod[1]
    t3 = low[3] + high[2] - far[2]
    s1 = low[4] + high[3] - far[3]
    s2 = low[2] + (low[3] - smooth_eps) - (5.0 / 3.0) * prod[2]
    s3 = low[1] + high[2] - far[1]
    third = [x * (1.0 / 3.0) for x in e]
    sixth = [x * (1.0 / 6.0) for x in e]
    left, keep_left = blend(
        m[2],
        (5.0 / 6.0) * e[1] - third[0],
        sixth[1] + third[2],
        (2.0 / 3.0) * e[2] - sixth[3],
        t1, t2, t3,
    )
    right, keep_right = blend(
        -m[3],
        (5.0 / 6.0) * e[3] - third[4],
        sixth[3] + third[2],
        (2.0 / 3.0) * e[2] - sixth[1],
        s1, s2, s3,
    )
    return jnp.maximum(left, 0.0), jnp.maximum(right, 0.0), e, keep_left, keep_right


def side_grads(factor, keep, e0, e1, e2, e3):
    offset, w1, w2, w3, r1, r2, r3, q1, q2, q3 = keep
    w1, w2, w3 = factor * w1, factor * w2, factor * w3
    k1 = (-2.0 * w1) * ((q1 - offset) * r1)
    k2 = (-2.0 * w2) * ((q2 - offset) * r2)
    k3 = (-2.0 * w3) * ((q3 - offset) * r3)
    g0 = k1 * ((8.0 / 3.0) * e0 - (11.0 / 3.0) * e1) - w1 * (1.0 / 3.0)
    g1 = (
        k1 * ((20.0 / 3.0) * e1 - (11.0 / 3.0) * e0)
        + k2 * ((8.0 / 3.0) * e1 - (5.0 / 3.0) * e2)
        + ((5.0 / 6.0) * w1 + (1.0 / 6.0) * w2)
    )
    g2 = (
        k2 * ((8.0 / 3.0) * e2 - (5.0 / 3.0) * e1)
        + k3 * ((20.0 / 3.0) * e2 - (11.0 / 3.0) * e3)
        + ((1.0 / 3.0) * w2 + (2.0 / 3.0) * w3)
    )
    g3 = k3 * ((8.0 / 3.0) * e3 - (11.0 / 3.0) * e2) - w3 * (1.0 / 6.0)
    return g0, g1, g2, g3


def cell_grads(part, inverse):
    left, right, e, keep_left, keep_right = part
    p, n = left * inverse, right * inverse
    a0, a1, a2, a3 = side_grads(p, keep_left, e[0], e[1], e[2], e[3])
    b0, b1, b2, b3 = side_grads(n, keep_right, e[4], e[3], e[2], e[1])
    ge = (a0, a1 + b3, a2 + b2, a3 + b1, b0)
    gm = (-ge[0], ge[0] - ge[1], ge[1] - ge[2] + p, ge[2] - ge[3] - n, ge[3] - ge[4], ge[4])
    return (-gm[0],) + tuple(gm[k] - gm[k + 1] for k in range(5)) + (gm[5],)


def kernel(
    sizes, level_ref, rate_ref, cot_ref, final_ref, rgrad_ref, igrad_ref,
    pad, coef, value, edge_out, edge_in, adj, mid, wgt, acc,
    row_out, row_in, col_out, col_in, send_sem, recv_sem,
):
    count_y, count_x = sizes
    rows, subs = level_ref.shape[0], level_ref.shape[1]
    own = pl.ds(8, subs)
    iy, ix = lax.axis_index("gy"), lax.axis_index("gx")
    prev_y = {"gy": lax.rem(iy + count_y - 1, count_y)}
    next_y = {"gy": lax.rem(iy + 1, count_y)}
    prev_x = {"gx": lax.rem(ix + count_x - 1, count_x)}
    next_x = {"gx": lax.rem(ix + 1, count_x)}
    targets = (prev_y, next_y, prev_x, next_x)

    barrier = pltpu.get_barrier_semaphore()
    for target in targets:
        pl.semaphore_signal(barrier, inc=1, device_id=target, device_id_type=pl.DeviceIdType.MESH)
    pl.semaphore_wait(barrier, 4)

    lane = lax.broadcasted_iota(jnp.int32, (subs, LANES), 1)
    sub = lax.broadcasted_iota(jnp.int32, (subs, LANES), 0)

    def copies(pairs, slot):
        return [
            pltpu.make_async_remote_copy(
                src_ref=source,
                dst_ref=target,
                send_sem=send_sem.at[slot, way],
                recv_sem=recv_sem.at[slot, way],
                device_id=targets[way],
                device_id_type=pl.DeviceIdType.MESH,
            )
            for way, (source, target) in enumerate(pairs)
        ]

    def state_copies(t, slot):
        return copies(
            (
                (pad.at[t, pl.ds(3, 3)], pad.at[t, pl.ds(3 + rows, 3)]),
                (pad.at[t, pl.ds(rows, 3)], pad.at[t, pl.ds(0, 3)]),
                (edge_out.at[t, 0], edge_in.at[t, 1]),
                (edge_out.at[t, 1], edge_in.at[t, 0]),
            ),
            slot,
        )

    def put(t, r, new):
        pad[t, 3 + r, own] = new
        edge_out[t, 0, pl.ds(r, 1)] = new[0:1]
        edge_out[t, 1, pl.ds(r, 1)] = new[subs - 1 : subs]

    def column_shift(here, before, after, k):
        if k < 0:
            return pltpu.roll(jnp.where(lane >= LANES + k, before, here), -k, 1)
        return pltpu.roll(jnp.where(lane < k, after, here), LANES - k, 1)

    def stage(t, slot, advance):
        moves = state_copies(t, slot)
        for move in moves:
            move.start()
        for move in moves:
            move.wait()
        pad[t, pl.ds(3, rows), 7] = edge_in[t, 0]
        pad[t, pl.ds(3, rows), 8 + subs] = edge_in[t, 1]

        def row(r, carry):
            here = pad[t, 3 + r, own]
            before = pad[t, 3 + r, pl.ds(7, subs)]
            after = pad[t, 3 + r, pl.ds(9, subs)]
            part_y = values([here if k == 3 else pad[t, r + k, own] for k in range(7)])
            part_x = values(
                [here if k == 0 else column_shift(here, before, after, k) for k in range(-3, 4)]
            )
            square = part_y[0] * part_y[0] + part_y[1] * part_y[1]
            square = square + part_x[0] * part_x[0] + part_x[1] * part_x[1]
            speed = jnp.sqrt(square + speed_floor)
            value[t, r] = speed
            advance(r, here, speed)
            inverse = 1.0 / speed
            grad_y = cell_grads(part_y, inverse)
            grad_x = cell_grads(part_x, inverse)
            for i, k in enumerate(SHIFTS):
                coef[t, i, r] = grad_y[k + 3]
                coef[t, 6 + i, r] = grad_x[k + 3]
            coef[t, 12, r] = grad_y[3] + grad_x[3]
            return carry

        lax.fori_loop(0, rows, row, 0)

    def first_row(r, carry):
        put(0, r, level_ref[r])
        return carry

    lax.fori_loop(0, rows, first_row, 0)

    def forward(step, carry):
        t = 2 * step

        def early(r, here, speed):
            put(t + 1, r, here - time_step * rate_ref[r] * speed)

        def late(r, here, speed):
            new = 0.5 * pad[t, 3 + r, own] + 0.5 * (here - time_step * rate_ref[r] * speed)
            put(t + 2, r, new)

        stage(t, 0, early)
        stage(t + 1, 1, late)
        return carry

    lax.fori_loop(0, STEPS, forward, 0)

    def pull_back(t, slot):
        def column(i):
            total = None
            for j, k in enumerate(SHIFTS):
                if 0 <= i - k < rows:
                    term = coef[t, j, i - k] * wgt[i - k]
                    total = term if total is None else total + term
            return total

        for k in range(3):
            row_out[t, 0, k] = column(k - 3)
            row_out[t, 1, k] = column(rows + k)
        moves = copies(
            (
                (row_out.at[t, 0], row_in.at[t, 1]),
                (row_out.at[t, 1], row_in.at[t, 0]),
                (col_out.at[t, 0], col_in.at[t, 1]),
                (col_out.at[t, 1], col_in.at[t, 0]),
            ),
            slot,
        )
        moves[0].start()
        moves[1].start()

        def row(r, carry):
            weight = wgt[r]
            total = coef[t, 12, r] * weight
            over = under = None
            for j, k in enumerate(SHIFTS):
                moved = pltpu.roll(coef[t, 6 + j, r] * weight, k % LANES, 1)
                outside = lane < k if k > 0 else lane >= LANES + k
                leaving = jnp.where(outside, moved, 0.0)
                total = total + jnp.where(outside, 0.0, moved)
                if k > 0:
                    over = leaving if over is None else over + leaving
                else:
                    under = leaving if under is None else under + leaving
            total = total + jnp.where(sub == 0, 0.0, pltpu.roll(over, 1, 0))
            total = total + jnp.where(sub == subs - 1, 0.0, pltpu.roll(under, subs - 1, 0))
            acc[r] = total
            col_out[t, 0, pl.ds(r, 1)] = under[0:1]
            col_out[t, 1, pl.ds(r, 1)] = over[subs - 1 : subs]
            return carry

        lax.fori_loop(0, rows, row, 0, unroll=2)
        moves[2].start()
        moves[3].start()
        for i in range(rows):
            acc[i] += column(i)
        for move in moves:
            move.wait()
        for k in range(3):
            acc[k] += row_in[t, 0, k]
            acc[rows - 3 + k] += row_in[t, 1, k]
        acc[:, 0] += col_in[t, 0]
        acc[:, subs - 1] += col_in[t, 1]

    def start_row(r, carry):
        final_ref[r] = pad[STAGES, 3 + r, own]
        adj[r] = cot_ref[r]
        rgrad_ref[r] = jnp.zeros((subs, LANES), jnp.float32)
        weight = (0.5 * time_step) * cot_ref[r]
        wgt[r] = rate_ref[r] * weight
        return carry

    lax.fori_loop(0, rows, start_row, 0)

    def backward(index, carry):
        t = 2 * (STEPS - 1 - index)
        pull_back(t + 1, 0)

        def late_row(r, inner):
            weight_late = (0.5 * time_step) * adj[r]
            middle = 0.5 * adj[r] - acc[r]
            weight = time_step * middle
            rgrad_ref[r] = rgrad_ref[r] - weight_late * value[t + 1, r] - weight * value[t, r]
            mid[r] = middle
            wgt[r] = rate_ref[r] * weight
            return inner

        lax.fori_loop(0, rows, late_row, 0, unroll=2)
        pull_back(t, 1)

        def early_row(r, inner):
            new = 0.5 * adj[r] + mid[r] - acc[r]
            adj[r] = new
            wgt[r] = rate_ref[r] * ((0.5 * time_step) * new)
            return inner

        lax.fori_loop(0, rows, early_row, 0, unroll=2)
        return carry

    lax.fori_loop(0, STEPS, backward, 0)

    def end_row(r, carry):
        igrad_ref[r] = adj[r]
        return carry

    lax.fori_loop(0, rows, end_row, 0)


def solution(mesh):
    sizes = (mesh.shape["gy"], mesh.shape["gx"])

    def shards(level_set, spread_rate, cotangent):
        rows, columns = level_set.shape
        subs = columns // LANES
        block = (rows, subs, LANES)
        f32 = jnp.float32
        outs = pl.pallas_call(
            functools.partial(kernel, sizes),
            out_shape=[jax.ShapeDtypeStruct(block, f32)] * 3,
            in_specs=[pl.BlockSpec(memory_space=pltpu.VMEM)] * 3,
            out_specs=[pl.BlockSpec(memory_space=pltpu.VMEM)] * 3,
            scratch_shapes=[
                pltpu.VMEM((STAGES + 1, rows + 6, subs + 16, LANES), f32),
                pltpu.VMEM((STAGES, 13) + block, f32),
                pltpu.VMEM((STAGES,) + block, f32),
                pltpu.VMEM((STAGES + 1, 2, rows, LANES), f32),
                pltpu.VMEM((STAGES, 2, rows, LANES), f32),
                pltpu.VMEM(block, f32),
                pltpu.VMEM(block, f32),
                pltpu.VMEM(block, f32),
                pltpu.VMEM(block, f32),
                pltpu.VMEM((STAGES, 2, 3, subs, LANES), f32),
                pltpu.VMEM((STAGES, 2, 3, subs, LANES), f32),
                pltpu.VMEM((STAGES, 2, rows, LANES), f32),
                pltpu.VMEM((STAGES, 2, rows, LANES), f32),
                pltpu.SemaphoreType.DMA((2, 4)),
                pltpu.SemaphoreType.DMA((2, 4)),
            ],
            compiler_params=pltpu.CompilerParams(
                collective_id=0, has_side_effects=True, vmem_limit_bytes=60 * 2**20
            ),
        )(*(x.reshape(block) for x in (level_set, spread_rate, cotangent)))
        return tuple(x.reshape(rows, columns) for x in outs)

    spec = P("gy", "gx")
    return jax.shard_map(
        shards, mesh=mesh, in_specs=(spec,) * 3, out_specs=(spec,) * 3, check_vma=False
    )
```
